32 devices in a mesh: rep: 8 (over y, x, core), shard: 4 (over z).
Axes of the slice: x: 2, y: 2, z: 4, core: 2. Of those that a mesh axis runs over, the one named last changes fastest.
Arguments:
- hidden_in: bfloat16 [16384, 1024], P(('rep', 'shard')), may hold values from -6 to 6
- seq_ids: int32 [16384], P(('rep', 'shard')), may hold values from 0 to 255, as said below
- positions: int32 [16384], P(('rep', 'shard')), may hold values from 0 to 1022, as said below
- cotangent: bfloat16 [16384, 1024], P(('rep', 'shard')), may hold values from -6 to 6
- weights: float32 [15360, 1024], P(None, 'shard')
- norm_gains: float32 [2304], P('shard')
- mom_one: float32 [15360, 1024], P(None, 'shard')
- mom_two: float32 [15360, 1024], P(None, 'shard')
- gain_mom_one: float32 [2304], P('shard')
- gain_mom_two: float32 [2304], P('shard')
Outputs:
- out_hidden: float32 [16384, 1024], P(('rep', 'shard'))
- grad_in: float32 [16384, 1024], P(('rep', 'shard'))
- weight_grad: float32 [15360, 1024], P('rep', 'shard')
- gain_grad: float32 [2304], P('shard')
- new_weights: float32 [15360, 1024], P(None, 'shard')
- new_gains: float32 [2304], P('shard')
- new_mom_one: float32 [15360, 1024], P('rep', 'shard')
- new_mom_two: float32 [15360, 1024], P('rep', 'shard')
- new_gain_mom_one: float32 [2304], P('shard')
- new_gain_mom_two: float32 [2304], P('shard')
The draws below stay inside these ranges and needn't reach their ends.
Inputs may be any that keep to these rules, and one draw needn't show every extreme that they name: `seq_ids`: within each device's pack of 512 tokens the ids start at 0 at its first token and rise by one where a new sequence begins, which happens only at an even place within the pack; a sequence never leaves its pack. Within a sequence the positions rise by one from token to token; a sequence's first position is at most 511.
All inputs are finite; a program needn't handle non-finite values.
Results may differ from the reference program's by a relative error of at most 0.012.
The reference program's roundings to bfloat16 on the way count: a program that leaves them out, or rounds other values in their place, can miss the bound.
Values may be sent and summed in bfloat16 or wider, within the bound.
No kernel may reach another device: no remote copies, remote signals or barrier semaphores. Data moves between devices by JAX's collectives and lax.ppermute only.
A program may use at most 384 MiB of HBM per device.

```python
import math
import jax
import jax.numpy as jnp
from jax import lax

D = 1024
HEADS = 16
KVH = 8
HD = 128
FF = 3072
TOK_DEV = 512
STEP = 3
QW = 2048
KVW = 1024
FLAT_R = 15360
GAINS = 2304
TOKENS = 16384


OUT_FAN_IN = 64.0


def pack_layout(key):
    pack_count = TOKENS // TOK_DEV
    column = jnp.arange(TOK_DEV, dtype=jnp.int32)[None, :]
    pack_row = jnp.arange(pack_count, dtype=jnp.int32)[:, None]
    even_place = column % 2 == 0
    start_marks = (jax.random.randint(jax.random.fold_in(key, 11), (pack_count, TOK_DEV), 0, max(TOK_DEV // 2, 2)) == 0) & even_place
    start_marks = start_marks | (column == 0)
    start_marks = jnp.where(pack_row == pack_count - 1, even_place, start_marks)
    start_marks = jnp.where(pack_row == 0, column == 0, start_marks)
    start_flags = start_marks.astype(jnp.int32)
    doc_ids = jnp.cumsum(start_flags, axis=1) - 1
    starts = lax.cummax(jnp.where(start_marks, column, 0), axis=1)
    offsets = jax.random.randint(jax.random.fold_in(key, 12), (pack_count, TOK_DEV), 0, 512)
    offsets = jnp.where(pack_row == 0, 511, offsets)
    first_pos = jnp.take_along_axis(offsets, starts, axis=1)
    return (doc_ids.reshape(TOKENS).astype(jnp.int32), (first_pos + column - starts).reshape(TOKENS).astype(jnp.int32))


def draw_seq_ids(key, part):
    return pack_layout(key)[0]


def draw_positions(key, part):
    return pack_layout(key)[1]


def segment_scale(segments):
    return jnp.concatenate([jnp.full((row_count,), row_factor, jnp.float32) for row_count, row_factor in segments])


def base_draw(key, shape):
    return jax.random.normal(key, shape, jnp.float32)


def matrix_grad_rows():
    token_root = math.sqrt(TOKENS)
    return [(QW, 0.4 * token_root), (KVW, 0.4 * token_root), (KVW, 0.7 * token_root), (QW, 0.25 * token_root), (2 * FF, 0.3 * token_root), (FF, 0.6 * token_root)]


def gain_grad_rows():
    token_root = math.sqrt(TOKENS)
    return [(D, 1.5 * token_root), (D, 0.8 * token_root), (HD, 1.5 * token_root), (HD, 1.2 * token_root)]


def spread_draw(key, shape):
    return jnp.exp(jax.random.uniform(key, shape, jnp.float32, math.log(0.3), math.log(3.0)))


def draw_weights(key, part):
    row_scale = segment_scale([(QW + 2 * KVW, D ** (-0.5)), (QW, OUT_FAN_IN ** (-0.5)), (2 * FF, D ** (-0.5)), (FF, FF ** (-0.5))])
    return base_draw(key, (FLAT_R, D)) * row_scale[:, None]


def draw_norm_gains(key, part):
    return 1.0 + 0.15 * jax.random.normal(key, (GAINS,), jnp.float32)


def draw_mom_one(key, part):
    row_scale = segment_scale(matrix_grad_rows()) * 0.1
    return base_draw(key, (FLAT_R, D)) * row_scale[:, None]


def draw_mom_two(key, part):
    row_scale = segment_scale(matrix_grad_rows())
    return spread_draw(key, (FLAT_R, D)) * (0.05 * row_scale * row_scale)[:, None]


def draw_gain_mom_one(key, part):
    return base_draw(key, (GAINS,)) * segment_scale(gain_grad_rows()) * 0.1


def draw_gain_mom_two(key, part):
    row_scale = segment_scale(gain_grad_rows())
    return spread_draw(key, (GAINS,)) * 0.05 * row_scale * row_scale


def levels(own_key, extent, cuts, low, top_value):
    def one(position, blocks):
        steps = jax.random.uniform(jax.random.fold_in(jax.random.fold_in(own_key, 6), position), (blocks,), jnp.float32, low / len(cuts), top_value / len(cuts))
        return jnp.repeat(jnp.exp(steps), extent[position] // blocks).reshape((-1,) + (1,) * (len(extent) - position - 1))

    gain = one(*cuts[0])
    for cut in cuts[1:]:
        gain = gain * one(*cut)
    return gain


def gaussian(key, extent, deviation, bound, split=(), held_as=jnp.bfloat16):
    result = deviation * jax.random.normal(key, extent, jnp.float32)
    if split:
        result = result * levels(key, extent, split, -0.22, 0.18)
    return jnp.clip(result, -bound, bound).astype(held_as)


def setup_inputs(seed: int = 0) -> dict:
    key_list = jax.random.split(jax.random.key(seed), 11)
    hidden_in = gaussian(key_list[0], (TOKENS, D), 1.0, 6.0, ((0, 32),))
    seq_ids = draw_seq_ids(jax.random.fold_in(key_list[10], 71), 0)
    positions = draw_positions(jax.random.fold_in(key_list[10], 71), 0)
    cotangent = gaussian(key_list[3], (TOKENS, D), 1.0, 6.0, ((0, 32),))
    weights = draw_weights(jax.random.fold_in(key_list[10], 71), 0)
    norm_gains = draw_norm_gains(jax.random.fold_in(key_list[10], 71), 0)
    mom_one = draw_mom_one(jax.random.fold_in(key_list[10], 71), 0)
    mom_two = draw_mom_two(jax.random.fold_in(key_list[10], 71), 0)
    gain_mom_one = draw_gain_mom_one(jax.random.fold_in(key_list[10], 71), 0)
    gain_mom_two = draw_gain_mom_two(jax.random.fold_in(key_list[10], 71), 0)
    return {"hidden_in": hidden_in, "seq_ids": seq_ids, "positions": positions, "cotangent": cotangent, "weights": weights, "norm_gains": norm_gains, "mom_one": mom_one, "mom_two": mom_two, "gain_mom_one": gain_mom_one, "gain_mom_two": gain_mom_two}


NORM_EPS = 1e-06
ROPE_THETA = 1000000.0
BETA_ONE = 0.9
BETA_TWO = 0.95
ADAM_EPS = 1e-08
RATE_MATRIX = 0.02
RATE_GAIN = 0.1
WEIGHT_DECAY = 0.1
PRECISE = lax.Precision.HIGHEST

@jax.custom_vjp
def low(v):
    return lax.optimization_barrier(v.astype(jnp.bfloat16)).astype(jnp.float32)

@jax.custom_vjp
def low_back(v):
    return v

def low_keep(v):
    return (low(v), None)

def low_pass(kept, grad):
    return (grad,)

def back_keep(v):
    return (v, None)

def back_low(kept, grad):
    return (low(grad),)
low.defvjp(low_keep, low_pass)
low_back.defvjp(back_keep, back_low)

def norm_gain(values, gain_vec):
    return values * lax.rsqrt(lax.optimization_barrier(jnp.mean(values * values, axis=-1, keepdims=True)) + NORM_EPS) * gain_vec

def rotary(values, cosine, sine_part):
    half_dim = values.shape[-1] // 2
    turned = jnp.concatenate([-values[..., half_dim:], values[..., :half_dim]], axis=-1)
    return values * cosine + turned * sine_part

def tables(positions):
    pair_count = HD // 2
    frequency = jnp.exp(jnp.arange(pair_count, dtype=jnp.float32) * (-2.0 * math.log(ROPE_THETA) / HD))
    angles = positions.astype(jnp.float32)[:, None] * frequency[None, :]
    cosine = jnp.cos(angles)
    sine_part = jnp.sin(angles)
    return (jnp.concatenate([cosine, cosine], axis=-1)[:, None, :], jnp.concatenate([sine_part, sine_part], axis=-1)[:, None, :])

def attend_block(inputs):
    queries, keys_all, values_all, doc_ids = inputs
    grouped = queries.reshape(TOK_DEV, KVH, HEADS // KVH, HD)
    raw_scores = jnp.einsum('qkgd,skd->kgqs', grouped, keys_all, precision=PRECISE) * HD ** (-0.5)
    raw_scores = low_back(raw_scores)
    place_idx = jnp.arange(TOK_DEV)
    allowed = (place_idx[:, None] >= place_idx[None, :]) & (doc_ids[:, None] == doc_ids[None, :])
    masked = jnp.where(allowed, raw_scores, -1e+30)
    row_max = lax.optimization_barrier(jnp.max(masked, axis=-1, keepdims=True))
    exp_scores = jnp.exp(masked - row_max)
    prob_low = low(exp_scores / lax.optimization_barrier(jnp.sum(exp_scores, axis=-1, keepdims=True)))
    mixture = jnp.einsum('kgqs,skd->qkgd', prob_low, values_all, precision=PRECISE)
    return mixture.reshape(TOK_DEV, HEADS * HD)

def forward(hidden, flat_all, gain_all, cosine, sine_part, doc_ids):
    qkv_w = flat_all[:QW + 2 * KVW]
    out_w = flat_all[QW + 2 * KVW:2 * QW + 2 * KVW]
    gate_up_w = flat_all[2 * QW + 2 * KVW:2 * QW + 2 * KVW + 2 * FF]
    down_w = flat_all[2 * QW + 2 * KVW + 2 * FF:]
    attn_gain = gain_all[:D]
    ffn_gain = gain_all[D:2 * D]
    query_gain = gain_all[2 * D:2 * D + HD]
    key_gain = gain_all[2 * D + HD:]
    normed = low(norm_gain(hidden, attn_gain))
    project = jnp.dot(normed, qkv_w.T, precision=PRECISE)
    queries_raw = low_back(project[:, :QW])
    keys_raw = low_back(project[:, QW:QW + KVW])
    values_raw = low_back(project[:, QW + KVW:])
    queries = low(rotary(norm_gain(queries_raw.reshape(TOKENS, HEADS, HD), query_gain), cosine, sine_part))
    keys_all = low(rotary(norm_gain(keys_raw.reshape(TOKENS, KVH, HD), key_gain), cosine, sine_part))
    values_all = low(values_raw).reshape(TOKENS, KVH, HD)
    pack_count = TOKENS // TOK_DEV
    attended = lax.map(jax.checkpoint(attend_block), (queries.reshape(pack_count, TOK_DEV, HEADS, HD), keys_all.reshape(pack_count, TOK_DEV, KVH, HD), values_all.reshape(pack_count, TOK_DEV, KVH, HD), doc_ids.reshape(pack_count, TOK_DEV)))
    attended = low(low_back(attended.reshape(TOKENS, QW)))
    branch = low_back(jnp.dot(attended, out_w, precision=PRECISE))
    middle = hidden + branch
    normed_two = low(norm_gain(middle, ffn_gain))
    gate_up = jnp.dot(normed_two, gate_up_w.T, precision=PRECISE)
    gate_part = low_back(gate_up[:, :FF])
    up_part = low_back(gate_up[:, FF:])
    inner_act = low(gate_part * jax.nn.sigmoid(gate_part) * up_part)
    return middle + low_back(jnp.dot(inner_act, down_w, precision=PRECISE))

def adamw_update(param_old, first_old, second_old, grad_now, rate_now, decay_now):
    first_new = BETA_ONE * first_old + (1.0 - BETA_ONE) * grad_now
    second_new = BETA_TWO * second_old + (1.0 - BETA_TWO) * grad_now * grad_now
    scaled_one = first_new / (1.0 - BETA_ONE ** STEP)
    scaled_two = second_new / (1.0 - BETA_TWO ** STEP)
    param_new = param_old - rate_now * (scaled_one / (jnp.sqrt(scaled_two) + ADAM_EPS) + decay_now * param_old)
    return (param_new, first_new, second_new)

def reference(hidden_in, seq_ids, positions, cotangent, weights, norm_gains, mom_one, mom_two, gain_mom_one, gain_mom_two):
    hidden = hidden_in.astype(jnp.float32)
    flat_all = low(weights)
    gain_all = low(norm_gains)
    cosine, sine_part = tables(positions)

    def layer_fn(hidden_x, flat_x, gain_x):
        return forward(hidden_x, flat_x, gain_x, cosine, sine_part, seq_ids)
    output, pullback = jax.vjp(layer_fn, hidden, flat_all, gain_all)
    grad_in, weight_grad, gain_grad = pullback(cotangent.astype(jnp.float32))
    new_weights, new_one, new_two = adamw_update(weights, mom_one, mom_two, weight_grad, RATE_MATRIX, WEIGHT_DECAY)
    new_gains, new_gone, new_gtwo = adamw_update(norm_gains, gain_mom_one, gain_mom_two, gain_grad, RATE_GAIN, 0.0)
    return (output, grad_in, weight_grad, gain_grad, new_weights, new_gains, new_one, new_two, new_gone, new_gtwo)
```

```python
import functools
import math

import jax
import jax.numpy as jnp
from jax import lax
from jax.experimental import pallas as pl
from jax.experimental.pallas import tpu as pltpu
from jax.sharding import PartitionSpec as P

D = 1024
HEADS = 16
KVH = 8
HD = 128
FF = 3072
STEP = 3
QW = 2048
KVW = 1024


NORM_EPS = 1e-06
ROPE_THETA = 1000000.0
BETA_ONE = 0.9
BETA_TWO = 0.95
ADAM_EPS = 1e-08
RATE_MATRIX = 0.02
RATE_GAIN = 0.1
WEIGHT_DECAY = 0.1


def norm_parts(values, gain_vec):
    inverse = lax.rsqrt(jnp.mean(values * values, axis=-1, keepdims=True) + NORM_EPS)
    unit_vec = values * inverse
    return (unit_vec, inverse, unit_vec * gain_vec)


def norm_back(grad_out, unit_vec, inverse, gain_vec):
    scaled = grad_out * gain_vec
    return inverse * (scaled - unit_vec * jnp.mean(scaled * unit_vec, axis=-1, keepdims=True))


def rotary(values, cosine, sine_part):
    half_dim = values.shape[-1] // 2
    turned = jnp.concatenate([-values[..., half_dim:], values[..., :half_dim]], axis=-1)
    return values * cosine + turned * sine_part


def rotary_back(grad_out, cosine, sine_part):
    half_dim = grad_out.shape[-1] // 2
    moved_part = grad_out * sine_part
    return grad_out * cosine + jnp.concatenate(
        [moved_part[..., half_dim:], -moved_part[..., :half_dim]], axis=-1
    )


def tables(positions):
    pair_count = HD // 2
    frequency = jnp.exp(
        jnp.arange(pair_count, dtype=jnp.float32) * (-2.0 * math.log(ROPE_THETA) / HD)
    )
    angles = positions.astype(jnp.float32)[:, None] * frequency[None, :]
    cosine = jnp.cos(angles)
    sine_part = jnp.sin(angles)
    return (
        jnp.concatenate([cosine, cosine], axis=-1)[:, None, :],
        jnp.concatenate([sine_part, sine_part], axis=-1)[:, None, :],
    )


def scores_of(grouped, keys_all, doc_ids, scale_factor):
    raw_scores = (
        jnp.einsum("qkgd,skd->kgqs", grouped, keys_all, preferred_element_type=jnp.float32)
        * scale_factor
    )
    place_idx = jnp.arange(doc_ids.shape[0])
    allowed = (place_idx[:, None] >= place_idx[None, :]) & (doc_ids[:, None] == doc_ids[None, :])
    return jnp.where(allowed, raw_scores, -1e30)


def adamw_update(param_old, first_old, second_old, grad_now, rate_now, decay_now):
    first_new = BETA_ONE * first_old + (1.0 - BETA_ONE) * grad_now
    second_new = BETA_TWO * second_old + (1.0 - BETA_TWO) * grad_now * grad_now
    scaled_one = first_new / (1.0 - BETA_ONE**STEP)
    scaled_two = second_new / (1.0 - BETA_TWO**STEP)
    param_new = param_old - rate_now * (
        scaled_one / (jnp.sqrt(scaled_two) + ADAM_EPS) + decay_now * param_old
    )
    return (param_new, first_new, second_new)


def contract_rows(left, right):
    return lax.dot_general(
        left, right, (((0,), (0,)), ((), ())), preferred_element_type=jnp.float32
    )


def contract_lanes(left, right):
    return lax.dot_general(
        left, right, (((1,), (1,)), ((), ())), preferred_element_type=jnp.float32
    )


def on_device(
    hidden_in,
    seq_ids,
    positions,
    cotangent,
    weights,
    norm_gains,
    mom_one,
    mom_two,
    gain_mom_one,
    gain_mom_two,
):
    flat_all, gain_low = (
        lax.all_gather(weights.astype(jnp.bfloat16), "shard", axis=1, tiled=True),
        lax.all_gather(norm_gains.astype(jnp.bfloat16), "shard", axis=0, tiled=True),
    )
    gain_all = gain_low.astype(jnp.float32)
    qkv_w = flat_all[: QW + 2 * KVW]
    out_w = flat_all[QW + 2 * KVW : 2 * QW + 2 * KVW]
    gate_up_w = flat_all[2 * QW + 2 * KVW : 2 * QW + 2 * KVW + 2 * FF]
    down_w = flat_all[2 * QW + 2 * KVW + 2 * FF :]
    attn_gain = gain_all[:D]
    ffn_gain = gain_all[D : 2 * D]
    query_gain = gain_all[2 * D : 2 * D + HD]
    key_gain = gain_all[2 * D + HD :]
    row_count = hidden_in.shape[0]
    group_size = HEADS // KVH
    scale_factor = 1.0 / math.sqrt(HD)
    hidden = hidden_in.astype(jnp.float32)
    cosine, sine_part = tables(positions)
    unit_one, inverse_one, pre_one = norm_parts(hidden, attn_gain)
    normed = pre_one.astype(jnp.bfloat16)
    project = contract_lanes(normed, qkv_w)
    query_unit, query_inv, query_pre = norm_parts(
        project[:, :QW].reshape(row_count, HEADS, HD), query_gain
    )
    key_unit, key_inv, key_pre = norm_parts(
        project[:, QW : QW + KVW].reshape(row_count, KVH, HD), key_gain
    )
    queries = rotary(query_pre, cosine, sine_part).astype(jnp.bfloat16)
    grouped = queries.reshape(row_count, KVH, group_size, HD)
    keys_all = rotary(key_pre, cosine, sine_part).astype(jnp.bfloat16)
    values_all = project[:, QW + KVW :].reshape(row_count, KVH, HD).astype(jnp.bfloat16)
    scores = scores_of(grouped, keys_all, seq_ids, scale_factor)
    row_max = jnp.max(scores, axis=-1, keepdims=True)
    exp_scores = jnp.exp(scores - row_max)
    exp_total = jnp.sum(exp_scores, axis=-1, keepdims=True)
    log_total = row_max + jnp.log(exp_total)
    prob_low = (exp_scores / exp_total).astype(jnp.bfloat16)
    attended = jnp.einsum(
        "kgqs,skd->qkgd", prob_low, values_all, preferred_element_type=jnp.float32
    )
    attended = attended.reshape(row_count, QW).astype(jnp.bfloat16)
    middle = hidden + jnp.dot(attended, out_w, preferred_element_type=jnp.float32)
    unit_two, inverse_two, pre_two = norm_parts(middle, ffn_gain)
    normed_two = pre_two.astype(jnp.bfloat16)
    gate_up = contract_lanes(normed_two, gate_up_w)
    gate_part = gate_up[:, :FF]
    up_part = gate_up[:, FF:]
    sigmoid_gate = jax.nn.sigmoid(gate_part)
    active = gate_part * sigmoid_gate
    inner_act = (active * up_part).astype(jnp.bfloat16)
    output = middle + jnp.dot(inner_act, down_w, preferred_element_type=jnp.float32)
    grad_out = cotangent.astype(jnp.float32)
    down_grad = contract_rows(inner_act, cotangent)
    inner_grad = contract_lanes(cotangent, down_w)
    gate_grad = (
        inner_grad * up_part * sigmoid_gate * (1.0 + gate_part * (1.0 - sigmoid_gate))
    ).astype(jnp.bfloat16)
    up_grad = (inner_grad * active).astype(jnp.bfloat16)
    gu_grad = jnp.concatenate([gate_grad, up_grad], axis=1)
    gate_up_grad = contract_rows(gu_grad, normed_two)
    normed_two_grad = jnp.dot(gu_grad, gate_up_w, preferred_element_type=jnp.float32)
    ffn_gain_grad = jnp.sum(normed_two_grad * unit_two, axis=0)
    middle_grad = grad_out + norm_back(normed_two_grad, unit_two, inverse_two, ffn_gain)
    branch_low = middle_grad.astype(jnp.bfloat16)
    out_grad = contract_rows(attended, branch_low)
    attended_grad = (
        contract_lanes(branch_low, out_w)
        .astype(jnp.bfloat16)
        .reshape(row_count, KVH, group_size, HD)
    )
    scores = scores_of(grouped, keys_all, seq_ids, scale_factor)
    prob_full = jnp.exp(scores - log_total)
    prob_again = prob_full.astype(jnp.bfloat16)
    value_grad = jnp.einsum(
        "kgqs,qkgd->skd", prob_again, attended_grad, preferred_element_type=jnp.float32
    )
    prob_grad = jnp.einsum(
        "qkgd,skd->kgqs", attended_grad, values_all, preferred_element_type=jnp.float32
    )
    row_delta = jnp.sum(prob_full * prob_grad, axis=-1, keepdims=True)
    score_grad = (prob_full * (prob_grad - row_delta)).astype(jnp.bfloat16)
    query_grad = jnp.einsum(
        "kgqs,skd->qkgd", score_grad, keys_all, preferred_element_type=jnp.float32
    )
    query_grad = query_grad.reshape(row_count, HEADS, HD) * scale_factor
    key_grad = (
        jnp.einsum("kgqs,qkgd->skd", score_grad, grouped, preferred_element_type=jnp.float32)
        * scale_factor
    )
    query_pre_grad = rotary_back(query_grad, cosine, sine_part)
    query_gain_grad = jnp.sum(query_pre_grad * query_unit, axis=(0, 1))
    query_raw_grad = norm_back(query_pre_grad, query_unit, query_inv, query_gain).reshape(
        row_count, QW
    )
    key_pre_grad = rotary_back(key_grad, cosine, sine_part)
    key_gain_grad = jnp.sum(key_pre_grad * key_unit, axis=(0, 1))
    key_raw_grad = norm_back(key_pre_grad, key_unit, key_inv, key_gain).reshape(row_count, KVW)
    qkv_grad = jnp.concatenate(
        [query_raw_grad, key_raw_grad, value_grad.reshape(row_count, KVW)], axis=1
    ).astype(jnp.bfloat16)
    qkv_w_grad = contract_rows(qkv_grad, normed)
    normed_grad = jnp.dot(qkv_grad, qkv_w, preferred_element_type=jnp.float32)
    attn_gain_grad = jnp.sum(normed_grad * unit_one, axis=0)
    grad_in = middle_grad + norm_back(normed_grad, unit_one, inverse_one, attn_gain)
    weight_term = jnp.concatenate([qkv_w_grad, out_grad, gate_up_grad, down_grad], axis=0)
    gain_term = jnp.concatenate(
        [attn_gain_grad, ffn_gain_grad, query_gain_grad, key_gain_grad], axis=0
    )
    rep_count = lax.axis_size("rep")
    shards = lax.axis_size("shard")
    rep_idx = lax.axis_index("rep")
    row_part = weight_term.shape[0] // rep_count
    row_start = rep_idx * row_part
    lane_part = weight_term.shape[1] // shards
    arranged = weight_term.reshape(rep_count, row_part, shards, lane_part).transpose(0, 2, 1, 3)
    arranged = arranged.reshape(rep_count * shards, row_part, lane_part)
    gain_part = gain_term.shape[0] // (rep_count * shards)
    gain_arranged = (
        gain_term.reshape(shards, rep_count, gain_part)
        .transpose(1, 0, 2)
        .reshape(rep_count * shards, gain_part)
    )
    weight_piece, gain_piece = (
        lax.psum_scatter(arranged, ("rep", "shard"), scatter_dimension=0, tiled=True),
        lax.psum_scatter(gain_arranged, ("rep", "shard"), scatter_dimension=0, tiled=True),
    )
    weight_piece = weight_piece[0]
    gain_piece = gain_piece[0]
    new_piece, new_one, new_two = adamw_update(
        lax.dynamic_slice_in_dim(weights, row_start, row_part, 0),
        lax.dynamic_slice_in_dim(mom_one, row_start, row_part, 0),
        lax.dynamic_slice_in_dim(mom_two, row_start, row_part, 0),
        weight_piece,
        RATE_MATRIX,
        WEIGHT_DECAY,
    )
    gain_start = rep_idx * gain_part
    new_gain_piece, gone_piece, gtwo_piece = adamw_update(
        lax.dynamic_slice_in_dim(norm_gains, gain_start, gain_part, 0),
        lax.dynamic_slice_in_dim(gain_mom_one, gain_start, gain_part, 0),
        lax.dynamic_slice_in_dim(gain_mom_two, gain_start, gain_part, 0),
        gain_piece,
        RATE_GAIN,
        0.0,
    )
    new_weights, new_gains, gain_grad, new_gone, new_gtwo = (
        lax.all_gather(new_piece.astype(jnp.bfloat16), "rep", axis=0, tiled=True).astype(
            new_piece.dtype
        ),
        lax.all_gather(new_gain_piece.astype(jnp.bfloat16), "rep", axis=0, tiled=True).astype(
            new_gain_piece.dtype
        ),
        lax.all_gather(gain_piece.astype(jnp.bfloat16), "rep", axis=0, tiled=True).astype(
            gain_piece.dtype
        ),
        lax.all_gather(gone_piece.astype(jnp.bfloat16), "rep", axis=0, tiled=True).astype(
            gone_piece.dtype
        ),
        lax.all_gather(gtwo_piece.astype(jnp.bfloat16), "rep", axis=0, tiled=True).astype(
            gtwo_piece.dtype
        ),
    )
    return (
        output,
        grad_in,
        weight_piece,
        gain_grad,
        new_weights,
        new_gains,
        new_one,
        new_two,
        new_gone,
        new_gtwo,
    )


BF = jnp.bfloat16
F32 = jnp.float32
TOK = 512
LANES = 256
FB = 384
ORDER_IN = (2, 1, 3)
ORDER_OUT = (0, 2, 1, 3)
SCALE = 1.0 / math.sqrt(HD)
ANY = pl.BlockSpec(memory_space=pl.ANY)
G_ROWS = 192
F_ROWS = 288


def swap_rep(value, bit):
    count = lax.axis_size("rep")
    return lax.ppermute(value, "rep", [(i, i ^ bit) for i in range(count)])


def swap_shard(value, bit):
    count = lax.axis_size("shard")
    return lax.ppermute(value, "shard", [(i, i ^ bit) for i in range(count)])


def call(kernel, ids, args, *, grid, in_specs, out_specs, out_shape, scratch=(), aliases=None, name, cost=None):
    spec = pltpu.PrefetchScalarGridSpec(
        num_scalar_prefetch=1,
        grid=grid,
        in_specs=in_specs,
        out_specs=out_specs,
        scratch_shapes=list(scratch),
    )
    return pl.pallas_call(
        kernel,
        grid_spec=spec,
        out_shape=out_shape,
        input_output_aliases=aliases or {},
        compiler_params=pltpu.CompilerParams(
            dimension_semantics=("arbitrary",) * len(grid), vmem_limit_bytes=56 << 20
        ),
        cost_estimate=cost,
        name=name,
    )(ids, *args)


def cost(flops, nbytes):
    return pl.CostEstimate(flops=int(flops), bytes_accessed=int(nbytes), transcendentals=0)


def fixed(shape):
    zeros = (0,) * len(shape)
    return pl.BlockSpec(shape, lambda *_: zeros)


def shape_of(shape, dtype):
    return jax.ShapeDtypeStruct(shape, dtype)


def dot_nt(left, right):
    return lax.dot_general(left, right, (((1,), (1,)), ((), ())), preferred_element_type=F32)


def dot_nn(left, right):
    return lax.dot_general(left, right, (((1,), (0,)), ((), ())), preferred_element_type=F32)


def dot_tn(left, right):
    return lax.dot_general(left, right, (((0,), (0,)), ((), ())), preferred_element_type=F32)


def pack_heads_kernel(ids, q, k, v, o, out):
    out[0, :, 0:64] = q[...].astype(BF).reshape(4, 64, LANES)
    out[0, :, 64:96] = k[...].astype(BF).reshape(4, 32, LANES)
    out[0, :, 96:128] = v[...].astype(BF).reshape(4, 32, LANES)
    out[0, :, 128:192] = o[...].astype(BF).reshape(4, 64, LANES)


def pack_heads(ids, weights):
    return call(
        pack_heads_kernel,
        ids,
        (weights,) * 4,
        grid=(4,),
        in_specs=[
            pl.BlockSpec((256, LANES), lambda i, s: (2 * i + s[0], 0)),
            pl.BlockSpec((128, LANES), lambda i, s: (16 + 2 * i + s[0], 0)),
            pl.BlockSpec((128, LANES), lambda i, s: (24 + 2 * i + s[0], 0)),
            pl.BlockSpec((256, LANES), lambda i, s: (16 + 2 * i + s[0], 0)),
        ],
        out_specs=pl.BlockSpec((1, 4, G_ROWS, LANES), lambda i, s: (i // 2, i % 2, 0, 0)),
        out_shape=shape_of((2, 8, G_ROWS, LANES), BF),
        name="pack_heads",
        cost=cost(0, 3072 * LANES * 6),
    )


def pack_ffn_kernel(ids, g, u, d, out):
    out[0, :, 0:96] = g[...].astype(BF).reshape(4, 96, LANES)
    out[0, :, 96:192] = u[...].astype(BF).reshape(4, 96, LANES)
    out[0, :, 192:288] = d[...].astype(BF).reshape(4, 96, LANES)


def pack_ffn(ids, weights):
    return call(
        pack_ffn_kernel,
        ids,
        (weights,) * 3,
        grid=(4,),
        in_specs=[
            pl.BlockSpec((FB, LANES), lambda i, s: (16 + 2 * i + s[0], 0)),
            pl.BlockSpec((FB, LANES), lambda i, s: (24 + 2 * i + s[0], 0)),
            pl.BlockSpec((FB, LANES), lambda i, s: (32 + 2 * i + s[0], 0)),
        ],
        out_specs=pl.BlockSpec((1, 4, F_ROWS, LANES), lambda i, s: (i // 2, i % 2, 0, 0)),
        out_shape=shape_of((2, 8, F_ROWS, LANES), BF),
        name="pack_ffn",
        cost=cost(0, 4608 * LANES * 6),
    )


def gather_chunk(packed, index, chip):
    rows = packed.shape[2]
    own = lax.dynamic_slice(packed, (index, 2 * chip, 0, 0), (1, 2, rows, LANES))[0]
    two = swap_shard(own, 2)
    pair = swap_shard(jnp.stack([own, two], axis=1), 1)
    part_a = jnp.concatenate([two[0][None], pair[0]], axis=0)
    part_b = jnp.concatenate([two[1][None], pair[1]], axis=0)
    x_a = swap_rep(part_a, 2)
    y_b = swap_rep(part_b, 4)
    y_a = swap_rep(jnp.stack([part_a, x_a]), 4)
    x_b = swap_rep(jnp.stack([part_b, y_b]), 2)
    return (packed, part_a, part_b, x_a, y_b, y_a, x_b)


def lanes_at(shard, k):
    return pl.ds(pl.multiple_of((shard ^ k) * LANES, LANES), LANES)


def assemble(ids, index, refs, full, sems):
    packed, part_a, part_b, x_a, y_b, y_a, x_b = refs
    chip = ids[1]
    shard = ids[2]
    moves = [(packed.at[index], full.at[:, :, lanes_at(shard, 0)])]
    for n, k in enumerate(ORDER_IN):
        for src, j, half in (
            (part_a.at[n], 0, 0),
            (part_b.at[n], 0, 1),
            (x_a.at[n], 1, 0),
            (x_b.at[0, n], 1, 1),
            (y_a.at[0, n], 2, 0),
            (y_b.at[n], 2, 1),
            (y_a.at[1, n], 3, 0),
            (x_b.at[1, n], 3, 1),
        ):
            moves.append((src, full.at[(chip ^ j) * 2 + half, :, lanes_at(shard, k)]))
    copies = [pltpu.make_async_copy(s, d, sems.at[i]) for i, (s, d) in enumerate(moves)]
    for copy in copies:
        copy.start()
    for copy in copies:
        copy.wait()


def send_out(ids, grads, refs, sems):
    send_a, keep_a, send_b, keep_b = refs
    chip = ids[1]
    shard = ids[2]
    moves = []
    for half, places in (
        (0, ((keep_a, 0, 0), (send_a, 0, 1), (keep_a, 1, 2), (send_a, 1, 3))),
        (1, ((keep_b, 0, 0), (keep_b, 1, 1), (send_b, 0, 2), (send_b, 1, 3))),
    ):
        for dst, slot, j in places:
            for n, k in enumerate(ORDER_OUT):
                moves.append((grads.at[(chip ^ j) * 2 + half, :, lanes_at(shard, k)], dst.at[slot, n]))
    copies = [pltpu.make_async_copy(s, d, sems.at[i]) for i, (s, d) in enumerate(moves)]
    for copy in copies:
        copy.start()
    for copy in copies:
        copy.wait()


def reduce_chunk(send_a, keep_a, send_b, keep_b):
    up = lambda t: t.astype(F32)
    in_a = swap_rep(send_a, 2)
    in_b = swap_rep(send_b, 4)
    next_a = swap_rep((up(keep_a[1]) + up(in_a[1])).astype(BF), 4)
    next_b = swap_rep((up(keep_b[1]) + up(in_b[1])).astype(BF), 2)
    total = jnp.stack(
        [up(keep_a[0]) + up(in_a[0]) + up(next_a), up(keep_b[0]) + up(in_b[0]) + up(next_b)]
    )
    in_z = swap_shard(total[:, 2:].astype(BF), 1)
    kept = total[:, :2] + up(in_z)
    last = swap_shard(kept[:, 1].astype(BF), 2)
    return (kept[:, 0] + up(last)).astype(BF)


def spread_chunk(piece):
    x_a = swap_rep(piece[0], 2)
    y_b = swap_rep(piece[1], 4)
    y_a = swap_rep(jnp.stack([piece[0], x_a]), 4)
    x_b = swap_rep(jnp.stack([piece[1], y_b]), 2)
    own = jnp.stack(
        [
            jnp.stack([piece[0], x_a, y_a[0], y_a[1]]),
            jnp.stack([piece[1], x_b[0], y_b, x_b[1]]),
        ]
    )
    return (own, swap_rep(own, 1))


def first_norm_kernel(ids, own, other, gain, out):
    for slot, ref in enumerate((own, other)):
        value = ref[...].astype(F32)
        inverse = lax.rsqrt(jnp.mean(value * value, axis=-1, keepdims=True) + NORM_EPS)
        out[slot] = (value * inverse * gain[...]).astype(BF)


def first_norm(ids, own, other, gain):
    block = pl.BlockSpec((128, D), lambda i, s: (i, 0))
    return call(
        first_norm_kernel,
        ids,
        (own, other, gain),
        grid=(4,),
        in_specs=[block, block, fixed((1, D))],
        out_specs=pl.BlockSpec((2, 128, D), lambda i, s: (0, i, 0)),
        out_shape=shape_of((2, TOK, D), BF),
        name="first_norm",
        cost=cost(0, 4 << 20),
    )


def head_rows(full, group, lo, hi):
    return full[pl.ds(4 * group, 4), lo:hi, :].reshape(4 * (hi - lo), D)


def head_norm(value):
    inverse = lax.rsqrt(jnp.mean(value * value, axis=-1, keepdims=True) + NORM_EPS)
    return value * inverse, inverse


def attn_fwd_kernel(index, first, ids, *refs):
    (h1, cosine, sine, bias, q_gain, k_gain), refs = refs[:6], refs[6:]
    pieces, refs = refs[:7], refs[7:]
    if not first:
        before, refs = refs[0], refs[1:]
    raw, qkv, mixed, logs, part, full, sems = refs
    group = pl.program_id(0)

    @pl.when(group == 0)
    def _():
        assemble(ids, index, pieces, full, sems)
        if first:
            part[...] = jnp.zeros_like(part)
        else:
            part[...] = before[...]

    w_qkv = jnp.concatenate(
        [
            head_rows(full, group, 0, 64),
            head_rows(full, group, 64, 96),
            head_rows(full, group, 96, 128),
        ],
        axis=0,
    )
    w_out = head_rows(full, group, 128, 192)
    for pack in range(2):
        rows = slice(pack * TOK, (pack + 1) * TOK)
        cos_t = cosine[pack]
        sin_t = sine[pack]
        project = dot_nt(h1[pack], w_qkv)
        raw[0, rows] = project[:, :FB]
        turned = []
        for part_idx, gain in ((0, q_gain), (1, q_gain), (2, k_gain)):
            unit, _ = head_norm(project[:, part_idx * HD : (part_idx + 1) * HD])
            scaled = unit * gain[...]
            turned.append((scaled * cos_t + pltpu.roll(scaled, HD // 2, 1) * sin_t).astype(BF))
        values = project[:, FB:].astype(BF)
        keys = turned[2]
        for n in range(3):
            qkv[0, rows, n * HD : (n + 1) * HD] = turned[n]
        qkv[0, rows, FB:] = values
        heads = []
        for head in range(2):
            blocks = []
            for block in range(2):
                span = (block + 1) * 256
                cols = slice(block * 256, span)
                scores = dot_nt(keys[:span], turned[head][cols]) * SCALE + bias[pack, :span, cols]
                top = jnp.max(scores, axis=0, keepdims=True)
                powers = jnp.exp(scores - top)
                total = jnp.sum(powers, axis=0, keepdims=True)
                probs = (powers * (1.0 / total)).astype(BF)
                logs[0, 2 * pack + head : 2 * pack + head + 1, cols] = top + jnp.log(total)
                blocks.append(dot_tn(values[:span], probs).T)
            heads.append(jnp.concatenate(blocks, axis=0).astype(BF))
        attended = jnp.concatenate(heads, axis=1)
        mixed[0, rows] = attended
        part[pack] += dot_nn(attended, w_out)


def attn_fwd(ids, index, h1, tables_in, gains, pieces, before):
    first = before is None
    args = [h1, *tables_in, *gains, *pieces]
    specs = [
        fixed((2, TOK, D)),
        fixed((2, TOK, HD)),
        fixed((2, TOK, HD)),
        fixed((2, TOK, TOK)),
        fixed((1, HD)),
        fixed((1, HD)),
    ] + [ANY] * 7
    aliases = {}
    if not first:
        args.append(before)
        specs.append(fixed((2, TOK, D)))
        aliases = {len(args): 4}
    return call(
        functools.partial(attn_fwd_kernel, index, first),
        ids,
        args,
        grid=(2,),
        in_specs=specs,
        out_specs=[
            pl.BlockSpec((1, 2 * TOK, FB), lambda g, s: (g, 0, 0)),
            pl.BlockSpec((1, 2 * TOK, 512), lambda g, s: (g, 0, 0)),
            pl.BlockSpec((1, 2 * TOK, 256), lambda g, s: (g, 0, 0)),
            pl.BlockSpec((1, 4, TOK), lambda g, s: (g, 0, 0)),
            fixed((2, TOK, D)),
        ],
        out_shape=[
            shape_of((2, 2 * TOK, FB), F32),
            shape_of((2, 2 * TOK, 512), BF),
            shape_of((2, 2 * TOK, 256), BF),
            shape_of((2, 4, TOK), F32),
            shape_of((2, TOK, D), F32),
        ],
        scratch=[pltpu.VMEM((8, G_ROWS, D), BF), pltpu.SemaphoreType.DMA((25,))],
        aliases=aliases,
        name=f"attn_fwd_{index}",
        cost=cost(8e9, 24 << 20),
    )


def attn_bwd_kernel(index, first, ids, *refs):
    (h1, own_dm, other_dm, cosine, sine, bias, q_gain, k_gain), refs = refs[:8], refs[8:]
    (raw, qkv, mixed, logs), refs = refs[:4], refs[4:]
    pieces, refs = refs[:7], refs[7:]
    if not first:
        before, refs = refs[0], refs[1:]
    outs, refs = refs[:4], refs[4:]
    dh1, gain_out, full, grads, d_qkv, sems, out_sems = refs
    group = pl.program_id(0)

    @pl.when(group == 0)
    def _():
        assemble(ids, index, pieces, full, sems)
        gain_out[...] = jnp.zeros_like(gain_out)
        if first:
            dh1[...] = jnp.zeros_like(dh1)
        else:
            dh1[...] = before[...]

    w_out = head_rows(full, group, 128, 192)
    for pack, d_mid in enumerate((own_dm, other_dm)):
        rows = slice(pack * TOK, (pack + 1) * TOK)
        cos_t = cosine[pack]
        sin_t = sine[pack]
        d_out = dot_nt(d_mid[...], w_out).astype(BF)
        keys = qkv[0, rows, 2 * HD : 3 * HD]
        values = qkv[0, rows, 3 * HD :]
        k_low = k_high = v_low = v_high = None
        queries_grad = []
        for head in range(2):
            queries = qkv[0, rows, head * HD : (head + 1) * HD]
            d_head = d_out[:, head * HD : (head + 1) * HD]
            blocks = []
            for block in range(2):
                span = (block + 1) * 256
                cols = slice(block * 256, span)
                scores = dot_nt(keys[:span], queries[cols]) * SCALE + bias[pack, :span, cols]
                probs = jnp.exp(scores - logs[0, 2 * pack + head : 2 * pack + head + 1, cols])
                d_probs = dot_nt(values[:span], d_head[cols])
                delta = jnp.sum(probs * d_probs, axis=0, keepdims=True)
                d_scores = (probs * (d_probs - delta)).astype(BF)
                v_part = dot_nn(probs.astype(BF), d_head[cols])
                k_part = dot_nn(d_scores, queries[cols])
                blocks.append(dot_tn(keys[:span], d_scores).T)
                v_low = v_part[:256] if v_low is None else v_low + v_part[:256]
                k_low = k_part[:256] if k_low is None else k_low + k_part[:256]
                if block == 1:
                    v_high = v_part[256:] if v_high is None else v_high + v_part[256:]
                    k_high = k_part[256:] if k_high is None else k_high + k_part[256:]
            queries_grad.append(jnp.concatenate(blocks, axis=0))
        keys_grad = jnp.concatenate([k_low, k_high], axis=0)
        values_grad = jnp.concatenate([v_low, v_high], axis=0)
        for n, (grad, gain, row) in enumerate(
            (
                (queries_grad[0], q_gain, 0),
                (queries_grad[1], q_gain, 0),
                (keys_grad, k_gain, 1),
            )
        ):
            grad = grad * SCALE
            grad = grad * cos_t - pltpu.roll(grad, HD // 2, 1) * sin_t
            unit, inverse = head_norm(raw[0, rows, n * HD : (n + 1) * HD])
            gain_out[row : row + 1, :] += jnp.sum(grad * unit, axis=0, keepdims=True)
            scaled = grad * gain[...]
            mean = jnp.mean(scaled * unit, axis=-1, keepdims=True)
            d_qkv[rows, n * HD : (n + 1) * HD] = (inverse * (scaled - unit * mean)).astype(BF)
        d_qkv[rows, FB:] = values_grad.astype(BF)
    w_qkv = jnp.concatenate(
        [
            head_rows(full, group, 0, 64),
            head_rows(full, group, 64, 96),
            head_rows(full, group, 96, 128),
        ],
        axis=0,
    )
    for pack in range(2):
        dh1[pack] += dot_nn(d_qkv[pack * TOK : (pack + 1) * TOK], w_qkv)
    d_w = dot_tn(d_qkv[...], h1[...].reshape(2 * TOK, D)).astype(BF)
    grads[pl.ds(4 * group, 4), 0:64, :] = d_w[:256].reshape(4, 64, D)
    grads[pl.ds(4 * group, 4), 64:96, :] = d_w[256:384].reshape(4, 32, D)
    grads[pl.ds(4 * group, 4), 96:128, :] = d_w[384:].reshape(4, 32, D)
    d_o = dot_tn(mixed[0, :TOK], own_dm[...]) + dot_tn(mixed[0, TOK:], other_dm[...])
    grads[pl.ds(4 * group, 4), 128:192, :] = d_o.astype(BF).reshape(4, 64, D)

    @pl.when(group == 1)
    def _():
        send_out(ids, grads, outs, out_sems)


def attn_bwd(ids, index, h1, d_mids, tables_in, gains, saved, pieces, before):
    first = before is None
    args = [h1, *d_mids, *tables_in, *gains, *saved, *pieces]
    specs = [
        fixed((2, TOK, D)),
        fixed((TOK, D)),
        fixed((TOK, D)),
        fixed((2, TOK, HD)),
        fixed((2, TOK, HD)),
        fixed((2, TOK, TOK)),
        fixed((1, HD)),
        fixed((1, HD)),
        pl.BlockSpec((1, 2 * TOK, FB), lambda g, s: (g, 0, 0)),
        pl.BlockSpec((1, 2 * TOK, 512), lambda g, s: (g, 0, 0)),
        pl.BlockSpec((1, 2 * TOK, 256), lambda g, s: (g, 0, 0)),
        pl.BlockSpec((1, 4, TOK), lambda g, s: (g, 0, 0)),
    ] + [ANY] * 7
    aliases = {}
    if not first:
        args.append(before)
        specs.append(fixed((2, TOK, D)))
        aliases = {len(args): 4}
    return call(
        functools.partial(attn_bwd_kernel, index, first),
        ids,
        args,
        grid=(2,),
        in_specs=specs,
        out_specs=[ANY] * 4 + [fixed((2, TOK, D)), fixed((8, HD))],
        out_shape=[shape_of((2, 4, G_ROWS, LANES), BF)] * 4
        + [shape_of((2, TOK, D), F32), shape_of((8, HD), F32)],
        scratch=[
            pltpu.VMEM((8, G_ROWS, D), BF),
            pltpu.VMEM((8, G_ROWS, D), BF),
            pltpu.VMEM((2 * TOK, 512), BF),
            pltpu.SemaphoreType.DMA((25,)),
            pltpu.SemaphoreType.DMA((32,)),
        ],
        aliases=aliases,
        name=f"attn_bwd_{index}",
        cost=cost(18e9, 30 << 20),
    )


def ffn_kernel(index, first, ids, *refs):
    (own_h, other_h, own_dy, other_dy), refs = refs[:4], refs[4:]
    pieces, refs = refs[:7], refs[7:]
    if not first:
        (out_before, dh_before), refs = refs[:2], refs[2:]
    outs, refs = refs[:4], refs[4:]
    out_part, dh_part, full, grads, h_all, dy_all, z_all, da_all, db_all, sems, out_sems = refs
    step = pl.program_id(0)

    @pl.when(step == 0)
    def _():
        assemble(ids, index, pieces, full, sems)
        h_all[:TOK] = own_h[...]
        h_all[TOK:] = other_h[...]
        dy_all[:TOK] = own_dy[...]
        dy_all[TOK:] = other_dy[...]
        if first:
            out_part[...] = jnp.zeros_like(out_part)
            dh_part[...] = jnp.zeros_like(dh_part)
        else:
            out_part[...] = out_before[...]
            dh_part[...] = dh_before[...]

    w_gate = head_rows(full, step, 0, 96)
    w_up = head_rows(full, step, 96, 192)
    w_down = head_rows(full, step, 192, 288)
    for pack in range(2):
        rows = slice(pack * TOK, (pack + 1) * TOK)
        gate = dot_nt(h_all[rows], w_gate)
        upper = dot_nt(h_all[rows], w_up)
        d_inner = dot_nt(dy_all[rows], w_down)
        sig = jax.nn.sigmoid(gate)
        active = gate * sig
        inner = (active * upper).astype(BF)
        d_gate = (d_inner * upper * sig * (1.0 + gate * (1.0 - sig))).astype(BF)
        d_up = (d_inner * active).astype(BF)
        z_all[rows] = inner
        da_all[rows] = d_gate
        db_all[rows] = d_up
        out_part[pack] += dot_nn(inner, w_down)
        dh_part[pack] += dot_nn(d_gate, w_gate) + dot_nn(d_up, w_up)
    at = pl.ds(4 * step, 4)
    grads[at, 0:96, :] = dot_tn(da_all[...], h_all[...]).astype(BF).reshape(4, 96, D)
    grads[at, 96:192, :] = dot_tn(db_all[...], h_all[...]).astype(BF).reshape(4, 96, D)
    grads[at, 192:288, :] = dot_tn(z_all[...], dy_all[...]).astype(BF).reshape(4, 96, D)

    @pl.when(step == 1)
    def _():
        send_out(ids, grads, outs, out_sems)


def ffn(ids, index, acts, pieces, before):
    first = before is None
    args = [*acts, *pieces]
    specs = [fixed((TOK, D))] * 4 + [ANY] * 7
    aliases = {}
    if not first:
        args += list(before)
        specs += [fixed((2, TOK, D))] * 2
        aliases = {len(args) - 1: 4, len(args): 5}
    return call(
        functools.partial(ffn_kernel, index, first),
        ids,
        args,
        grid=(2,),
        in_specs=specs,
        out_specs=[ANY] * 4 + [fixed((2, TOK, D))] * 2,
        out_shape=[shape_of((2, 4, F_ROWS, LANES), BF)] * 4 + [shape_of((2, TOK, D), F32)] * 2,
        scratch=[
            pltpu.VMEM((8, F_ROWS, D), BF),
            pltpu.VMEM((8, F_ROWS, D), BF),
            pltpu.VMEM((2 * TOK, D), BF),
            pltpu.VMEM((2 * TOK, D), BF),
            pltpu.VMEM((2 * TOK, FB), BF),
            pltpu.VMEM((2 * TOK, FB), BF),
            pltpu.VMEM((2 * TOK, FB), BF),
            pltpu.SemaphoreType.DMA((25,)),
            pltpu.SemaphoreType.DMA((32,)),
        ],
        aliases=aliases,
        name=f"ffn_{index}",
        cost=cost(14.5e9, 30 << 20),
    )


ROWS = pl.BlockSpec((128, D), lambda i, s: (i, 0))
PACK0 = pl.BlockSpec((1, 128, D), lambda i, s: (0, i, 0))


def middle_kernel(ids, hidden, own, other, gain, mid, h2):
    value = hidden[...].astype(F32) + (own[0] + other[...])
    mid[...] = value
    inverse = lax.rsqrt(jnp.mean(value * value, axis=-1, keepdims=True) + NORM_EPS)
    h2[...] = (value * inverse * gain[...]).astype(BF)


def middle(ids, hidden, parts, other, gain):
    return call(
        middle_kernel,
        ids,
        (hidden, parts, other, gain),
        grid=(4,),
        in_specs=[ROWS, PACK0, ROWS, fixed((1, D))],
        out_specs=[ROWS, ROWS],
        out_shape=[shape_of((TOK, D), F32), shape_of((TOK, D), BF)],
        name="middle",
        cost=cost(0, 8 << 20),
    )


def norm_grad_kernel(low, ids, base, own, other, values, gain, grad, *rest):
    gain_grad = rest[-1]
    value = values[...].astype(F32)
    inverse = lax.rsqrt(jnp.mean(value * value, axis=-1, keepdims=True) + NORM_EPS)
    unit = value * inverse
    upstream = own[0] + other[...]

    @pl.when(pl.program_id(0) == 0)
    def _():
        gain_grad[...] = jnp.zeros_like(gain_grad)

    gain_grad[...] += jnp.sum(upstream * unit, axis=0, keepdims=True)
    scaled = upstream * gain[...]
    mean = jnp.mean(scaled * unit, axis=-1, keepdims=True)
    result = base[...].astype(F32) + inverse * (scaled - unit * mean)
    grad[...] = result
    if low:
        rest[0][...] = result.astype(BF)


def norm_grad(ids, base, parts, other, values, gain, low, name):
    outs = [shape_of((TOK, D), F32)] + ([shape_of((TOK, D), BF)] if low else [])
    return call(
        functools.partial(norm_grad_kernel, low),
        ids,
        (base, parts, other, values, gain),
        grid=(4,),
        in_specs=[ROWS, PACK0, ROWS, ROWS, fixed((1, D))],
        out_specs=[ROWS] * len(outs) + [fixed((1, D))],
        out_shape=outs + [shape_of((1, D), F32)],
        name=name,
        cost=cost(0, 10 << 20),
    )


def adam_rows(grad, weight, first, second):
    new_weight, new_first, new_second = adamw_update(
        weight, first, second, grad, RATE_MATRIX, WEIGHT_DECAY
    )
    return new_weight, new_first, new_second


def adam_store(ids, kept, outs, sems, block, unit, per_owner, count):
    for n in range(count):
        number = block * count + n

        @pl.when(number // per_owner == ids[3])
        def _(n=n, number=number):
            row = pl.multiple_of((number - per_owner * ids[3]) * unit, unit)
            copies = [
                pltpu.make_async_copy(
                    kept.at[i, pl.ds(n * unit, unit)], outs[i].at[pl.ds(row, unit)], sems.at[i]
                )
                for i in range(3)
            ]
            for copy in copies:
                copy.start()
            for copy in copies:
                copy.wait()


def adam_ffn_kernel(index, first, ids, own, other, weight, one, two, *refs):
    if not first:
        refs = refs[4:]
    new, grad_out, one_out, two_out, kept, sems = refs
    block = pl.program_id(0)
    part = pl.program_id(1)
    core = ids[0]
    for parity in range(2):
        for t in range(4):
            at = (t % 2, (2 * block + t // 2) ^ ids[1], pl.ds(pl.multiple_of(part * 96, 32), 96))
            grad = jnp.where(core == parity, own[at].astype(F32), other[at].astype(F32))
            rows = slice(parity * FB + t * 96, parity * FB + t * 96 + 96)
            fresh, fresh_one, fresh_two = adam_rows(grad, weight[rows], one[rows], two[rows])
            new[rows] = fresh
            kept[0, rows] = grad
            kept[1, rows] = fresh_one
            kept[2, rows] = fresh_two
    adam_store(
        ids, kept, (grad_out, one_out, two_out), sems, 8 + 4 * part + 2 * index + block, FB, 5, 2
    )


def adam_heads_kernel(index, first, ids, own, other, weight, one, two, *refs):
    if not first:
        refs = refs[4:]
    new, grad_out, one_out, two_out, kept, sems = refs
    group = pl.program_id(0)
    part = pl.program_id(1)
    core = ids[0]

    def pieces(parity, lo, size, start):
        for t in range(4):
            at = (t % 2, (2 * group + t // 2) ^ ids[1], slice(lo, lo + size))
            grad = jnp.where(core == parity, own[at].astype(F32), other[at].astype(F32))
            rows = slice(start + t * size, start + (t + 1) * size)
            fresh, fresh_one, fresh_two = adam_rows(grad, weight[rows], one[rows], two[rows])
            new[rows] = fresh
            kept[0, rows] = grad
            kept[1, rows] = fresh_one
            kept[2, rows] = fresh_two

    for s, todo in enumerate(
        (
            ((0, 0, 64, 0),),
            ((1, 0, 64, 0),),
            ((0, 64, 32, 0), (1, 64, 32, 128)),
            ((0, 96, 32, 0), (1, 96, 32, 128)),
            ((0, 128, 64, 0),),
            ((1, 128, 64, 0),),
        )
    ):

        @pl.when(part == s)
        def _(todo=todo):
            for item in todo:
                pieces(*item)

    adam_store(
        ids, kept, (grad_out, one_out, two_out), sems, head_block(index, group, part), 128, 15, 2
    )


def head_block(index, group, part):
    head = 2 * index + group
    return jnp.where(
        part < 2,
        2 * head + part,
        jnp.where(part < 4, 8 + 4 * (part - 2) + head, 16 + 2 * head + part - 4),
    )


def adam(ids, heads, index, grads, state, before):
    first = before is None
    if heads:
        rows, steps, kernel = 256, 6, adam_heads_kernel
        place = lambda b, p, s: (head_block(index, b, p), 0)
    else:
        rows, steps, kernel = 768, 3, adam_ffn_kernel
        place = lambda b, p, s: (8 + 4 * p + 2 * index + b, 0)
    block = pl.BlockSpec((rows, LANES), place)
    args = [*grads, *state]
    specs = [fixed(grads[0].shape)] * 2 + [block] * 3
    aliases = {}
    if not first:
        args += list(before)
        specs += [ANY] * 4
        aliases = {len(args) - 3 + i: i for i in range(4)}
    piece = state[0].shape[0] // 8
    return call(
        functools.partial(kernel, index, first),
        ids,
        args,
        grid=(2, steps),
        in_specs=specs,
        out_specs=[block, ANY, ANY, ANY],
        out_shape=[shape_of(state[0].shape, F32)] + [shape_of((piece, LANES), F32)] * 3,
        scratch=[pltpu.VMEM((3, rows, LANES), F32), pltpu.SemaphoreType.DMA((3,))],
        aliases=aliases,
        name=f"adam_{'heads' if heads else 'ffn'}_{index}",
        cost=cost(0, rows * steps * 2 * LANES * 18),
    )


def all_sum(value):
    for bit in (1, 2, 4):
        value = value + swap_rep(value, bit)
    for bit in (1, 2):
        value = value + swap_shard(value, bit)
    return value


def on_device_fast(
    hidden_in,
    seq_ids,
    positions,
    cotangent,
    weights,
    norm_gains,
    mom_one,
    mom_two,
    gain_mom_one,
    gain_mom_two,
):
    rep = lax.axis_index("rep")
    shard = lax.axis_index("shard")
    chip = rep // 2
    ids = jnp.stack([rep % 2, chip, shard, rep]).astype(jnp.int32)

    heads_w = pack_heads(ids, weights)
    w_attn = [gather_chunk(heads_w, 0, chip), gather_chunk(heads_w, 1, chip)]
    ffn_w = pack_ffn(ids, weights)
    w_ffn = [gather_chunk(ffn_w, 0, chip), gather_chunk(ffn_w, 1, chip)]

    gain_own = norm_gains.astype(BF)
    gain_two = swap_shard(gain_own, 2)
    gain_pair = swap_shard(jnp.stack([gain_own, gain_two]), 1)
    relative = jnp.stack([gain_own, gain_pair[0], gain_two, gain_pair[1]]).astype(F32)
    gain_all = jnp.concatenate(
        [lax.dynamic_index_in_dim(relative, n ^ shard, 0, keepdims=False) for n in range(4)]
    )
    attn_gain = gain_all[:D][None]
    ffn_gain = gain_all[D : 2 * D][None]
    head_gains = (gain_all[2 * D : 2 * D + HD][None], gain_all[2 * D + HD :][None])

    hidden_other = swap_rep(hidden_in, 1)
    cot_other = swap_rep(cotangent, 1)
    marks = jnp.stack([seq_ids, positions])
    marks_other = swap_rep(marks, 1)
    seqs = jnp.stack([seq_ids, marks_other[0]])
    places = jnp.stack([positions, marks_other[1]])
    frequency = jnp.exp(
        jnp.arange(HD // 2, dtype=F32) * (-2.0 * math.log(ROPE_THETA) / HD)
    )
    angles = places.astype(F32)[:, :, None] * frequency
    cos_half = jnp.cos(angles)
    sin_half = jnp.sin(angles)
    cosine = jnp.concatenate([cos_half, cos_half], axis=-1)
    sine = jnp.concatenate([-sin_half, sin_half], axis=-1)
    order = jnp.arange(TOK)
    allowed = (order[:, None] <= order[None, :])[None] & (seqs[:, :, None] == seqs[:, None, :])
    bias = jnp.where(allowed, 0.0, -1e30).astype(F32)
    tables_in = (cosine, sine, bias)

    h1 = first_norm(ids, hidden_in, hidden_other, attn_gain)
    *saved_0, part = attn_fwd(ids, 0, h1, tables_in, head_gains, w_attn[0], None)
    *saved_1, part = attn_fwd(ids, 1, h1, tables_in, head_gains, w_attn[1], part)
    mid, h2 = middle(ids, hidden_in, part, swap_rep(part[1], 1), ffn_gain)
    acts = (h2, swap_rep(h2, 1), cotangent, cot_other)
    *sent_f0, out_part, dh_part = ffn(ids, 0, acts, w_ffn[0], None)
    *sent_f1, out_part, dh_part = ffn(ids, 1, acts, w_ffn[1], (out_part, dh_part))
    d_mid, d_low, ffn_gain_grad = norm_grad(
        ids, cotangent, dh_part, swap_rep(dh_part[1], 1), mid, ffn_gain, True, "mid_grad"
    )
    output = mid + out_part[0] + swap_rep(out_part[1], 1)
    d_mids = (d_low, swap_rep(d_low, 1))
    *sent_a1, dh1, head_gain_1 = attn_bwd(
        ids, 1, h1, d_mids, tables_in, head_gains, saved_1, w_attn[1], None
    )
    *sent_a0, dh1, head_gain_0 = attn_bwd(
        ids, 0, h1, d_mids, tables_in, head_gains, saved_0, w_attn[0], dh1
    )
    grad_in, attn_gain_grad = norm_grad(
        ids, d_mid, dh1, swap_rep(dh1[1], 1), hidden_in, attn_gain, False, "in_grad"
    )

    state = (weights, mom_one, mom_two)
    result = None
    for heads, index, sent in (
        (False, 0, sent_f0),
        (False, 1, sent_f1),
        (True, 1, sent_a1),
        (True, 0, sent_a0),
    ):
        grads = spread_chunk(reduce_chunk(*sent))
        result = adam(ids, heads, index, grads, state, result)
    new_weights, weight_grad, new_one, new_two = result

    head_gain = head_gain_0 + head_gain_1
    gain_term = jnp.concatenate(
        [attn_gain_grad[0], ffn_gain_grad[0], head_gain[0], head_gain[1]]
    ).reshape(18, 128)
    gain_sum = all_sum(gain_term).reshape(-1)
    size = norm_gains.shape[0]
    gain_grad = lax.dynamic_slice_in_dim(gain_sum, shard * size, size, 0)
    new_gains, new_gone, new_gtwo = adamw_update(
        norm_gains, gain_mom_one, gain_mom_two, gain_grad, RATE_GAIN, 0.0
    )
    return (
        output,
        grad_in,
        weight_grad,
        gain_grad,
        new_weights,
        new_gains,
        new_one,
        new_two,
        new_gone,
        new_gtwo,
    )


def solution(mesh):
    return jax.shard_map(
        on_device_fast if dict(mesh.shape) == {"rep": 8, "shard": 4} else on_device,
        mesh=mesh,
        in_specs=(
            P(("rep", "shard"), None),
            P(("rep", "shard")),
            P(("rep", "shard")),
            P(("rep", "shard"), None),
            P(None, "shard"),
            P("shard"),
            P(None, "shard"),
            P(None, "shard"),
            P("shard"),
            P("shard"),
        ),
        out_specs=(
            P(("rep", "shard"), None),
            P(("rep", "shard"), None),
            P("rep", "shard"),
            P("shard"),
            P(None, "shard"),
            P("shard"),
            P("rep", "shard"),
            P("rep", "shard"),
            P("shard"),
            P("shard"),
        ),
        check_vma=False,
    )
```
